256 devices in a mesh: dp: 16 (over z, y_lo), tensor: 4 (over x), section: 4 (over y_hi, core).
Axes of the slice: x: 4, y: 4 (y_hi: 2, y_lo: 2; y = y_hi * 2 + y_lo), z: 8, core: 2. Of those that a mesh axis runs over, the one named last changes fastest.
Arguments:
- grad_parts: bfloat16 [4, 16, 4, 1024, 1024], P('section', 'dp', None, None, 'tensor'), may hold values from -1.5 to 1.5
- first_moment: float32 [4, 4, 1024, 1024], P('section', 'tensor', 'dp'), may hold values from -3 to 3
- second_moment: float32 [4, 4, 1024, 1024], P('section', 'tensor', 'dp'), may hold values from 0.1 to 4
- left_stat: float32 [4, 4, 1024, 1024], P('section', 'tensor', 'dp'), may hold values from -12288 to 184320
- right_stat: float32 [4, 4, 1024, 1024], P('section', 'tensor', 'dp'), may hold values from -12288 to 184320
- left_basis: float32 [4, 4, 1024, 1024], P('section', 'tensor', 'dp'), may hold values from -0.1875 to 0.1875
- right_basis: float32 [4, 4, 1024, 1024], P('section', 'tensor', 'dp'), may hold values from -0.1875 to 0.1875
- gain_grads: float32 [4, 16, 4, 2, 1024], P('section', 'dp', 'tensor'), may hold values from -1.2 to 1.2
- gain_first: float32 [4, 2, 1024], P('section'), may hold values from -3 to 3
- gain_second: float32 [4, 2, 1024], P('section'), may hold values from 0.1 to 4
- table_grads: float32 [4, 16, 32, 16], P('section', 'dp', None, 'tensor'), may hold values from -1.2 to 1.2
- table_first: float32 [32, 16], P(None, 'tensor'), may hold values from -3 to 3
- table_second: float32 [32, 16], P(None, 'tensor'), may hold values from 0.1 to 4
Outputs:
- update: float32 [4, 4, 1024, 1024], P('section', 'tensor', 'dp')
- first_next: float32 [4, 4, 1024, 1024], P('section', 'tensor', 'dp')
- second_next: float32 [4, 4, 1024, 1024], P('section', 'tensor', 'dp')
- left_next: float32 [4, 4, 1024, 1024], P('section', 'tensor', 'dp')
- right_next: float32 [4, 4, 1024, 1024], P('section', 'tensor', 'dp')
- left_rotation: float32 [4, 4, 1024, 1024], P('section', 'tensor', 'dp')
- right_rotation: float32 [4, 4, 1024, 1024], P('section', 'tensor', 'dp')
- gain_update: float32 [4, 2, 1024], P('section')
- gain_moment: float32 [4, 2, 1024], P('section')
- gain_squares: float32 [4, 2, 1024], P('section')
- table_update: float32 [32, 16], P(None, 'tensor')
- table_moment: float32 [32, 16], P(None, 'tensor')
- table_squares: float32 [32, 16], P(None, 'tensor')
The draws below stay inside these ranges and needn't reach their ends.
All inputs are finite; a program needn't handle non-finite values.
Results may differ from the reference program's by a relative error of at most 0.014.
Values may be sent and summed in bfloat16 or wider, within the bound.
A program may use at most 64 MiB of HBM per device.

```python
import math
import jax
import jax.numpy as jnp
from jax import lax

D = 1024
HEADS = 16
BUCKETS = 32
MATS = 4
NORMS = 2
NS_ITERS = 3
LAYERS = 4
N_DP = 16
N_TENSOR = 4


def order_of(subkey):
    return jax.random.permutation(subkey, D)


def statistic(key):
    first_key, second_key, third_key = jax.random.split(key, 3)
    base = jax.random.uniform(first_key, (LAYERS, MATS, D, D), jnp.float32, -1.7, 1.7)
    symmetric = 0.5 * (base + jnp.swapaxes(base, -1, -2))
    factor = jax.random.uniform(second_key, (LAYERS, MATS, D), jnp.float32, 1.0, 1.5)
    order_keys = jax.random.split(third_key, LAYERS * MATS)
    ranks = jax.vmap(order_of)(order_keys).reshape(LAYERS, MATS, D)
    scales = factor / jnp.sqrt(ranks.astype(jnp.float32) + 1.0)
    identity = (jnp.arange(D)[:, None] == jnp.arange(D)[None, :]).astype(jnp.float32)
    inner = symmetric * (1.4 / math.sqrt(D)) + 3.0 * identity
    return inner * scales[..., :, None] * scales[..., None, :] * (24.0 * D)


def draw_left_stat(key, part):
    return statistic(jax.random.fold_in(key, 11))


def draw_right_stat(key, part):
    return statistic(jax.random.fold_in(key, 23))


def with_spikes(values, rng, source, target, blocks, factor):
    owner, partner = [(jnp.arange(values.shape[dim]) // (values.shape[dim] // blocks)).reshape([-1 if axis == dim else 1 for axis in range(values.ndim)]) for dim in (source, target)]
    chosen = jax.random.permutation(rng, blocks)[partner]
    strong = (owner == chosen) | (owner == (partner + blocks // 2) % blocks)
    return jnp.where(strong, factor * values, values)


def block_levels(key, dims, cuts, least, top_value):
    loudness = 1.0
    for dim, parts in cuts:
        steps = jax.random.uniform(jax.random.fold_in(jax.random.fold_in(key, 6), dim), (parts,), jnp.float32, least / len(cuts), top_value / len(cuts))
        loudness = loudness * jnp.repeat(jnp.exp(steps), dims[dim] // parts).reshape((-1,) + (1,) * (len(dims) - 1 - dim))
    return loudness


def normal_values(rng, extent, deviation, most, pieces=(), kind=jnp.bfloat16):
    array = jax.random.normal(rng, extent, jnp.float32) * deviation
    if len(pieces) > 0:
        array = block_levels(rng, extent, pieces, -0.22, 0.18) * array
    return jnp.clip(array, min=-most, max=most).astype(kind)


def noise_with(own_key, extent, scale, bound, shards, heavy, kind=jnp.bfloat16):
    drawn = scale * jax.random.normal(own_key, extent, jnp.float32)
    if shards:
        drawn = drawn * block_levels(own_key, extent, shards, -0.22, 0.18)
    return jnp.clip(with_spikes(drawn, jax.random.fold_in(own_key, 3), *heavy), -bound, bound).astype(kind)


def setup_inputs(seed: int = 0) -> dict:
    seeds = jax.random.split(jax.random.key(seed), 14)
    return {
        "grad_parts": noise_with(seeds[0], (LAYERS, N_DP, MATS, D, D), 0.25, 1.5, ((0, 4), (1, 16), (4, 4)), (1, 3, 16, 2.0)),
        "first_moment": normal_values(seeds[1], (LAYERS, MATS, D, D), 0.5, 3.0, ((0, 4), (1, 4), (2, 16)), jnp.float32),
        "second_moment": jnp.clip(jnp.exp(math.log(4.0) - 3.6888794 * jax.random.uniform(seeds[2], (LAYERS, MATS, D, D), jnp.float32) ** block_levels(seeds[2], (LAYERS, MATS, D, D), ((0, 4), (1, 4), (2, 16)), -0.2, 0.2)), 0.1, 4.0),
        "left_stat": draw_left_stat(jax.random.fold_in(seeds[13], 71), 0),
        "right_stat": draw_right_stat(jax.random.fold_in(seeds[13], 71), 0),
        "left_basis": normal_values(seeds[5], (LAYERS, MATS, D, D), D ** -0.5, 0.1875, ((0, 4), (1, 4), (2, 16)), jnp.float32),
        "right_basis": normal_values(seeds[6], (LAYERS, MATS, D, D), D ** -0.5, 0.1875, ((0, 4), (1, 4), (2, 16)), jnp.float32),
        "gain_grads": normal_values(seeds[7], (LAYERS, N_DP, N_TENSOR, NORMS, D), 0.2, 1.2, ((0, 4), (1, 16), (2, 4)), jnp.float32),
        "gain_first": normal_values(seeds[8], (LAYERS, NORMS, D), 0.5, 3.0, ((0, 4),), jnp.float32),
        "gain_second": jnp.clip(jnp.exp(math.log(4.0) - 3.6888794 * jax.random.uniform(seeds[9], (LAYERS, NORMS, D), jnp.float32) ** block_levels(seeds[9], (LAYERS, NORMS, D), ((0, 4),), -0.2, 0.2)), 0.1, 4.0),
        "table_grads": normal_values(seeds[10], (LAYERS, N_DP, BUCKETS, HEADS), 0.2, 1.2, ((0, 4), (1, 16), (3, 4)), jnp.float32),
        "table_first": normal_values(seeds[11], (BUCKETS, HEADS), 0.5, 3.0, ((1, 4),), jnp.float32),
        "table_second": jnp.clip(jnp.exp(math.log(4.0) - 3.6888794 * jax.random.uniform(seeds[12], (BUCKETS, HEADS), jnp.float32) ** block_levels(seeds[12], (BUCKETS, HEADS), ((1, 4),), -0.2, 0.2)), 0.1, 4.0),
    }


beta_first = 0.9
beta_second = 0.95
beta_stat = 0.95
adam_eps = 1e-08
norm_eps = 1e-06
step_count = 10.0

def product(left, right):
    return jnp.dot(left, right, preferred_element_type=jnp.float32)

def to_half(value):
    return value.astype(jnp.bfloat16)

def adam_direction(first, second):
    first_hat = first / (1.0 - beta_first ** step_count)
    second_hat = second / (1.0 - beta_second ** step_count)
    return first_hat / (jnp.sqrt(second_hat) + adam_eps)

def orthogonalize(power):
    iterate = power / jnp.sqrt(jnp.sum(power * power) + norm_eps)
    for sweep in range(NS_ITERS):
        iterate_half = to_half(iterate)
        gram = to_half(product(iterate_half, iterate_half.T))
        iterate = 1.5 * iterate - 0.5 * product(gram, iterate_half)
    return iterate

def reference(grad_parts, first_moment, second_moment, left_stat, right_stat, left_basis, right_basis, gain_grads, gain_first, gain_second, table_grads, table_first, table_second):

    def one_matrix(index):
        layer = index // MATS
        which = index % MATS
        grad_half = to_half(lax.optimization_barrier(jnp.sum(grad_parts[layer, :, which].astype(jnp.float32), axis=0)))
        left_half = to_half(left_basis[layer, which])
        right_half = to_half(right_basis[layer, which])
        rotated_half = to_half(product(grad_half, right_half))
        rotated = product(left_half.T, rotated_half)
        first_new = beta_first * first_moment[layer, which] + (1.0 - beta_first) * rotated
        second_new = beta_second * second_moment[layer, which] + (1.0 - beta_second) * rotated * rotated
        direction = to_half(adam_direction(first_new, second_new))
        back_half = to_half(product(left_half, direction))
        update = product(back_half, right_half.T)
        left_new = beta_stat * left_stat[layer, which] + product(grad_half, grad_half.T)
        right_new = beta_stat * right_stat[layer, which] + product(grad_half.T, grad_half)
        left_rotation = orthogonalize(product(to_half(left_new), left_half))
        right_rotation = orthogonalize(product(to_half(right_new), right_half))
        return (update, first_new, second_new, left_new, right_new, left_rotation, right_rotation)
    results = lax.map(one_matrix, jnp.arange(LAYERS * MATS, dtype=jnp.int32))
    shaped = [item.reshape(LAYERS, MATS, D, D) for item in results]
    gain_sum = lax.optimization_barrier(jnp.sum(gain_grads, axis=(1, 2)))
    gain_moment = beta_first * gain_first + (1.0 - beta_first) * gain_sum
    gain_squares = beta_second * gain_second + (1.0 - beta_second) * gain_sum * gain_sum
    gain_update = adam_direction(gain_moment, gain_squares)
    table_sum = lax.optimization_barrier(jnp.sum(table_grads, axis=(0, 1)))
    table_moment = beta_first * table_first + (1.0 - beta_first) * table_sum
    table_squares = beta_second * table_second + (1.0 - beta_second) * table_sum * table_sum
    table_update = adam_direction(table_moment, table_squares)
    return (shaped[0], shaped[1], shaped[2], shaped[3], shaped[4], shaped[5], shaped[6], gain_update, gain_moment, gain_squares, table_update, table_moment, table_squares)
```

```python
import jax
import jax.numpy as jnp
from jax import lax
from jax.experimental import pallas as pl
from jax.experimental.pallas import tpu as pltpu
from jax.sharding import PartitionSpec as P

MESH = pl.DeviceIdType.MESH
F32, BF16 = jnp.float32, jnp.bfloat16

beta_first = 0.9
beta_second = 0.95
beta_stat = 0.95
adam_eps = 1e-08
norm_eps = 1e-06
step_count = 10.0

D = 1024
NZ = 8
BLK = D // NZ
ROWS = BLK // 2
COLS = D // 4
HALF = D // 2
TILE = 256


def adam_direction(first, second):
    first_hat = first / (1.0 - beta_first**step_count)
    second_hat = second / (1.0 - beta_second**step_count)
    return first_hat / (jnp.sqrt(second_hat) + adam_eps)


def dot_nn(a, b):
    return jnp.dot(a, b, preferred_element_type=F32)


def dot_nt(a, b):
    return lax.dot_general(a, b, (((1,), (1,)), ((), ())), preferred_element_type=F32)


def dot_tn(a, b):
    return lax.dot_general(a, b, (((0,), (0,)), ((), ())), preferred_element_type=F32)


def wrap(value, size):
    return lax.rem(value + 2 * size, size)


def kernel(
    g, m1, m2, ls, rs, lb, rb, gg, gf, gs, tg, tf, ts,
    o_update, o_first, o_second, o_left, o_right, o_lrot, o_rrot,
    o_gu, o_gm, o_gs, o_tu, o_tm, o_ts,
    left128, basis_send, basis, grad, xhalf, xa, xb, gram, xf, ehalf,
    rs_recv, rs_send, zsum, ysum, gx, stat_recv, next_half,
    s_buf, rot, rot_send, d128, e_send, upd_send, upd_recv, fin_send, fin_recv,
    gain_x, gain_y, gain_ys, gain_z, tab_s, tab_y, tab_ys, tab_z,
    ring_ss, ring_rs, y_ss, y_rs, x_ss, x_rs, small_ss, small_rs, sring_ss, sring_rs,
):
    dp = lax.axis_index("dp")
    x = lax.axis_index("tensor")
    sec = lax.axis_index("section")
    z = dp // 2
    y = lax.rem(dp, 2)
    up = {"dp": wrap(z + 1, NZ) * 2 + y}
    down = {"dp": wrap(z - 1, NZ) * 2 + y}
    partner = {"dp": z * 2 + 1 - y}
    pending = []

    def remote(src, dst, ssem, rsem, device):
        return pltpu.make_async_remote_copy(
            src_ref=src, dst_ref=dst, send_sem=ssem, recv_sem=rsem,
            device_id=device, device_id_type=MESH,
        )

    def send(*spec):
        copy = remote(*spec)
        copy.start()
        pending.append(copy)

    def xpeer(k):
        return {"tensor": lax.rem(x + k, 4)}

    def speer(k):
        return {"section": lax.rem(sec + k, 4)}

    barrier = pltpu.get_barrier_semaphore()
    peers = [up, down, partner] + [xpeer(k) for k in (1, 2, 3)] + [speer(k) for k in (1, 2, 3)]
    for peer in peers:
        pl.semaphore_signal(barrier, inc=1, device_id=peer, device_id_type=MESH)
    pl.semaphore_wait(barrier, len(peers))

    def rows(block, sub):
        return pl.ds(pl.multiple_of(block * BLK + sub * ROWS, ROWS), ROWS)

    def blk(block):
        return pl.ds(pl.multiple_of(block * BLK, BLK), BLK)

    mine = blk(z)
    own_sub = pl.ds(pl.multiple_of(y * ROWS, ROWS), ROWS)

    def ring_spec(phase, buf, direction, m, at_sender):
        step = m // 2
        swapped = (m % 2 == 1) if m < 6 else (direction == 1)
        sub = (1 - y) if swapped else y
        sign = -1 if direction == 0 else 1
        origin = z if at_sender else z + sign
        block = wrap(origin + sign * step, NZ)
        part = buf.at[rows(block, sub), :]
        device = up if direction == 0 else down
        return (
            part, part, ring_ss.at[phase, direction, m], ring_rs.at[phase, direction, m], device,
        )

    def ring_send(phase, buf, m):
        for direction in (0, 1):
            send(*ring_spec(phase, buf, direction, m, True))

    def ring_wait(phase, buf, m):
        for direction in (0, 1):
            remote(*ring_spec(phase, buf, direction, m, False)).wait_recv()

    def ring_step(phase, buf, m):
        ring_wait(phase, buf, m)
        if m < 4:
            ring_send(phase, buf, m + 2)
        elif m == 4:
            send(*ring_spec(phase, buf, 0, 6, True))
        elif m == 5:
            send(*ring_spec(phase, buf, 1, 6, True))

    def rs_chunk(direction, step):
        return wrap(z - 1 - step if direction == 0 else z + 1 + step, NZ)

    def rs_copy(direction, step, src):
        send(
            src, rs_recv.at[direction, step], ring_ss.at[0, direction, step],
            ring_rs.at[0, direction, step], up if direction == 0 else down,
        )

    for direction in (0, 1):
        rs_copy(direction, 0, g.at[pl.ds(2 * direction, 2), blk(rs_chunk(direction, 0)), :])

    lhalf = lb[...].astype(BF16)
    rhalf = rb[...].astype(BF16)
    left128[own_sub, :] = lhalf

    @pl.when(y == 0)
    def _():
        basis[rows(z, 0), :] = lhalf
        basis_send[...] = rhalf

    @pl.when(y == 1)
    def _():
        basis[rows(z, 1), :] = rhalf
        basis_send[...] = lhalf

    send(basis_send, basis.at[rows(z, y), :], y_ss.at[0], y_rs.at[0], partner)
    ring_send(1, basis, 0)
    send(left128.at[own_sub, :], left128.at[own_sub, :], y_ss.at[1], y_rs.at[1], partner)

    def stat_copy(src):
        return remote(src, stat_recv, y_ss.at[2], y_rs.at[2], partner)

    @pl.when(y == 0)
    def _():
        stat_copy(rs).start()

    @pl.when(y == 1)
    def _():
        stat_copy(ls).start()

    pending.append(stat_copy(ls))

    for k in (1, 2, 3):
        send(gg, gain_x.at[x], small_ss.at[0, k], small_rs.at[0, k], xpeer(k))
        send(tg, tab_s.at[sec], small_ss.at[1, k], small_rs.at[1, k], speer(k))
    gain_x[x] = gg[...]
    tab_s[sec] = tg[...]

    remote(basis_send, basis.at[rows(z, 1 - y), :], y_ss.at[0], y_rs.at[0], partner).wait_recv()
    ring_send(1, basis, 1)

    for m in range(7):
        for direction in (0, 1):
            chunk = rs_chunk(direction, m + 1)
            remote(
                rs_recv.at[direction, m], rs_recv.at[direction, m], ring_ss.at[0, direction, m],
                ring_rs.at[0, direction, m], up if direction == 0 else down,
            ).wait_recv()
            own = g[pl.ds(2 * direction, 2), blk(chunk), :].astype(F32)
            total = (rs_recv[direction, m].astype(F32) + own).astype(BF16)
            if m < 6:
                rs_send[direction, m] = total
                rs_copy(direction, m + 1, rs_send.at[direction, m])
            else:
                zsum[pl.ds(2 * direction, 2)] = total
        ring_step(1, basis, m)

    send(zsum, ysum, y_ss.at[3], y_rs.at[3], partner)
    remote(zsum, ysum, y_ss.at[3], y_rs.at[3], partner).wait_recv()
    gx[...] = (zsum[...].astype(F32) + ysum[...].astype(F32)).astype(BF16)

    def cols(rank):
        return pl.ds(pl.multiple_of(rank * COLS, COLS), COLS)

    for k in (1, 2, 3):
        send(gx.at[lax.rem(x + k, 4)], grad.at[mine, cols(x)], x_ss.at[k], x_rs.at[k], xpeer(k))
    grad[mine, cols(x)] = gx[x]

    for k in (1, 2, 3):
        source = wrap(x - k, 4)
        remote(gg, gain_x.at[source], small_ss.at[0, k], small_rs.at[0, k], xpeer(k)).wait_recv()
        source = wrap(sec - k, 4)
        remote(tg, tab_s.at[source], small_ss.at[1, k], small_rs.at[1, k], speer(k)).wait_recv()
    gain_ys[...] = gain_x[0] + gain_x[1] + gain_x[2] + gain_x[3]
    tab_ys[...] = tab_s[0] + tab_s[1] + tab_s[2] + tab_s[3]
    send(gain_ys, gain_y, small_ss.at[0, 0], small_rs.at[0, 0], partner)
    send(tab_ys, tab_y, small_ss.at[1, 0], small_rs.at[1, 0], partner)

    for k in (1, 2, 3):
        source = wrap(x - k, 4)
        part = grad.at[mine, cols(source)]
        remote(gx.at[0], part, x_ss.at[k], x_rs.at[k], xpeer(k)).wait_recv()

    ring_send(2, grad, 0)
    ring_send(2, grad, 1)
    remote(gain_ys, gain_y, small_ss.at[0, 0], small_rs.at[0, 0], partner).wait_recv()
    remote(tab_ys, tab_y, small_ss.at[1, 0], small_rs.at[1, 0], partner).wait_recv()
    gain_z[z] = gain_ys[...] + gain_y[...]
    tab_z[z] = tab_ys[...] + tab_y[...]

    def small_ring(m, at_sender):
        origin = z if at_sender else z - 1
        slot = wrap(origin - m, NZ)
        first = (gain_z.at[slot], gain_z.at[slot], sring_ss.at[0, m], sring_rs.at[0, m], up)
        second = (tab_z.at[slot], tab_z.at[slot], sring_ss.at[1, m], sring_rs.at[1, m], up)
        return first, second

    for m in range(7):
        ring_step(2, grad, m)

    remote(ls, stat_recv, y_ss.at[2], y_rs.at[2], partner).wait_recv()

    @pl.when(y == 0)
    def _():
        prod = dot_nt(grad[mine, :], grad[...])
        top = beta_stat * ls[...] + prod[:ROWS]
        o_left[...] = top
        next_half[:ROWS] = top.astype(BF16)
        next_half[ROWS:] = (beta_stat * stat_recv[...] + prod[ROWS:]).astype(BF16)

    @pl.when(y == 1)
    def _():
        prod = dot_tn(grad[:, mine], grad[...])
        bottom = beta_stat * rs[...] + prod[ROWS:]
        o_right[...] = bottom
        next_half[:ROWS] = (beta_stat * stat_recv[...] + prod[:ROWS]).astype(BF16)
        next_half[ROWS:] = bottom.astype(BF16)

    xhalf[mine, :] = dot_nn(next_half[...], basis[...]).astype(BF16)
    ring_send(3, xhalf, 0)
    ring_send(3, xhalf, 1)

    s_copy = remote(s_buf, s_buf, y_ss.at[4], y_rs.at[4], partner)
    rot_copy = remote(rot_send, rot, y_ss.at[5], y_rs.at[5], partner)
    d_copy = remote(
        d128.at[pl.ds(0, ROWS), :], d128.at[pl.ds(0, ROWS), :], y_ss.at[6], y_rs.at[6], partner
    )
    e_copy = remote(e_send, ehalf.at[mine, :], y_ss.at[7], y_rs.at[7], partner)

    for spec in small_ring(0, True):
        send(*spec)

    def small_step(m):
        for spec in small_ring(m, False):
            remote(*spec).wait_recv()
        if m < 6:
            for spec in small_ring(m + 1, True):
                send(*spec)

    @pl.when(y == 0)
    def _():
        s_buf[...] = dot_tn(basis[:, mine], grad[...]).astype(BF16)
        s_copy.start()
        prod = dot_tn(grad[:, mine], grad[...])
        o_right[...] = beta_stat * rs[...] + prod[:ROWS]

    @pl.when(y == 1)
    def _():
        prod = dot_nt(grad[rows(z, 1), :], grad[...])
        o_left[...] = beta_stat * ls[...] + prod

    ring_step(3, xhalf, 0)
    small_step(0)
    ring_step(3, xhalf, 1)
    small_step(1)

    @pl.when(y == 1)
    def _():
        s_copy.wait_recv()
        rotated = dot_nn(s_buf[...], basis[...])
        rot_send[...] = rotated[:ROWS]
        rot_copy.start()
        rot[...] = rotated[ROWS:]

    ring_step(3, xhalf, 2)
    small_step(2)

    @pl.when(y == 0)
    def _():
        rot_copy.wait_recv()

    rotated = rot[...]
    first_new = beta_first * m1[...] + (1.0 - beta_first) * rotated
    second_new = beta_second * m2[...] + (1.0 - beta_second) * rotated * rotated
    o_first[...] = first_new
    o_second[...] = second_new
    d128[own_sub, :] = adam_direction(first_new, second_new).astype(BF16)

    @pl.when(y == 0)
    def _():
        d_copy.start()

    ring_step(3, xhalf, 3)
    small_step(3)
    ring_step(3, xhalf, 4)
    small_step(4)

    @pl.when(y == 1)
    def _():
        d_copy.wait_recv()
        e_send[...] = dot_nt(d128[...], basis[pl.ds(0, HALF), :]).astype(BF16)
        e_copy.start()
        ehalf[mine, :] = dot_nt(d128[...], basis[pl.ds(HALF, HALF), :]).astype(BF16)

    ring_step(3, xhalf, 5)
    small_step(5)

    @pl.when(y == 0)
    def _():
        e_copy.wait_recv()

    ring_send(4, ehalf, 0)
    ring_send(4, ehalf, 1)
    ring_step(3, xhalf, 6)
    small_step(6)

    def tile(i):
        return pl.ds(pl.multiple_of(i * TILE, TILE), TILE)

    def squares(i, acc):
        part = xhalf[tile(i), :].astype(F32)
        return acc + jnp.sum((part * part).reshape(TILE // 8, 8, D), axis=0)

    partial = lax.fori_loop(0, D // TILE, squares, jnp.zeros((8, D), F32))
    scale = 1.0 / jnp.sqrt(jnp.sum(partial, keepdims=True) + norm_eps)

    @pl.loop(0, D // TILE)
    def _(i):
        value = xhalf[tile(i), :].astype(F32) * scale
        xf[tile(i), :] = value
        xa[tile(i), :] = value.astype(BF16)

    def gram_pass(source):
        @pl.loop(0, D // TILE)
        def _(i):
            gram[tile(i), :] = dot_nt(source[tile(i), :], source[...]).astype(BF16)

    def apply_pass(source, target):
        @pl.loop(0, D // TILE)
        def _(i):
            value = 1.5 * xf[tile(i), :] - 0.5 * dot_nn(gram[tile(i), :], source[...])
            xf[tile(i), :] = value
            target[tile(i), :] = value.astype(BF16)

    ring_step(4, ehalf, 0)
    gram_pass(xa)
    ring_step(4, ehalf, 1)
    ring_step(4, ehalf, 2)
    apply_pass(xa, xb)
    ring_step(4, ehalf, 3)
    ring_step(4, ehalf, 4)
    gram_pass(xb)
    ring_step(4, ehalf, 5)
    apply_pass(xb, xa)
    ring_step(4, ehalf, 6)

    gram_own = dot_nt(xa[mine, :], xa[...]).astype(BF16)
    final = 1.5 * xf[mine, :] - 0.5 * dot_nn(gram_own, xa[...])

    @pl.when(y == 0)
    def _():
        o_lrot[...] = final[:ROWS]
        fin_send[...] = final[ROWS:].astype(BF16)

    @pl.when(y == 1)
    def _():
        o_rrot[...] = final[ROWS:]
        fin_send[...] = final[:ROWS].astype(BF16)

    send(fin_send, fin_recv, y_ss.at[8], y_rs.at[8], partner)

    remote(
        left128.at[own_sub, :], left128.at[pl.ds(pl.multiple_of((1 - y) * ROWS, ROWS), ROWS), :],
        y_ss.at[1], y_rs.at[1], partner,
    ).wait_recv()

    @pl.when(y == 0)
    def _():
        upd = dot_nn(left128[...], ehalf[...])
        o_update[:, :HALF] = upd[:ROWS]
        upd_send[...] = upd[ROWS:]

    @pl.when(y == 1)
    def _():
        upd = dot_nn(left128[...], ehalf[...])
        o_update[:, HALF:] = upd[ROWS:]
        upd_send[...] = upd[:ROWS]

    send(upd_send, upd_recv, y_ss.at[9], y_rs.at[9], partner)

    def total_of(slots):
        total = slots[0]
        for k in range(1, NZ):
            total = total + slots[k]
        return total

    gain_sum = total_of(gain_z)
    gain_moment = beta_first * gf[...] + (1.0 - beta_first) * gain_sum
    gain_squares = beta_second * gs[...] + (1.0 - beta_second) * gain_sum * gain_sum
    o_gm[...] = gain_moment
    o_gs[...] = gain_squares
    o_gu[...] = adam_direction(gain_moment, gain_squares)
    table_sum = total_of(tab_z)
    table_moment = beta_first * tf[...] + (1.0 - beta_first) * table_sum
    table_squares = beta_second * ts[...] + (1.0 - beta_second) * table_sum * table_sum
    o_tm[...] = table_moment
    o_ts[...] = table_squares
    o_tu[...] = adam_direction(table_moment, table_squares)

    remote(fin_send, fin_recv, y_ss.at[8], y_rs.at[8], partner).wait_recv()
    remote(upd_send, upd_recv, y_ss.at[9], y_rs.at[9], partner).wait_recv()

    @pl.when(y == 0)
    def _():
        o_rrot[...] = fin_recv[...].astype(F32)
        o_update[:, HALF:] = upd_recv[...]
        s_copy.wait_send()
        d_copy.wait_send()

    @pl.when(y == 1)
    def _():
        o_lrot[...] = fin_recv[...].astype(F32)
        o_update[:, :HALF] = upd_recv[...]
        rot_copy.wait_send()
        e_copy.wait_send()

    for copy in pending:
        copy.wait_send()


def local(
    grad_parts, first_moment, second_moment, left_stat, right_stat, left_basis, right_basis,
    gain_grads, gain_first, gain_second, table_grads, table_first, table_second,
):
    wide = jax.ShapeDtypeStruct((ROWS, D), F32)
    gain = jax.ShapeDtypeStruct((2, D), F32)
    table = jax.ShapeDtypeStruct((32, 4), F32)
    vmem = pl.BlockSpec(memory_space=pltpu.VMEM)
    dma = pltpu.SemaphoreType.DMA
    outs = pl.pallas_call(
        kernel,
        out_shape=[wide] * 7 + [gain] * 3 + [table] * 3,
        in_specs=[vmem] * 13,
        out_specs=[vmem] * 13,
        scratch_shapes=[
            pltpu.VMEM((BLK, D), BF16),
            pltpu.VMEM((ROWS, D), BF16),
            pltpu.VMEM((D, D), BF16),
            pltpu.VMEM((D, D), BF16),
            pltpu.VMEM((D, D), BF16),
            pltpu.VMEM((D, D), BF16),
            pltpu.VMEM((D, D), BF16),
            pltpu.VMEM((D, D), BF16),
            pltpu.VMEM((D, D), F32),
            pltpu.VMEM((D, HALF), BF16),
            pltpu.VMEM((2, 7, 2, BLK, COLS), BF16),
            pltpu.VMEM((2, 6, 2, BLK, COLS), BF16),
            pltpu.VMEM((4, BLK, COLS), BF16),
            pltpu.VMEM((4, BLK, COLS), BF16),
            pltpu.VMEM((4, BLK, COLS), BF16),
            pltpu.VMEM((ROWS, D), F32),
            pltpu.VMEM((BLK, D), BF16),
            pltpu.VMEM((BLK, D), BF16),
            pltpu.VMEM((ROWS, D), F32),
            pltpu.VMEM((ROWS, D), F32),
            pltpu.VMEM((BLK, D), BF16),
            pltpu.VMEM((BLK, HALF), BF16),
            pltpu.VMEM((ROWS, HALF), F32),
            pltpu.VMEM((ROWS, HALF), F32),
            pltpu.VMEM((ROWS, D), BF16),
            pltpu.VMEM((ROWS, D), BF16),
            pltpu.VMEM((4, 2, D), F32),
            pltpu.VMEM((2, D), F32),
            pltpu.VMEM((2, D), F32),
            pltpu.VMEM((NZ, 2, D), F32),
            pltpu.VMEM((4, 32, 4), F32),
            pltpu.VMEM((32, 4), F32),
            pltpu.VMEM((32, 4), F32),
            pltpu.VMEM((NZ, 32, 4), F32),
            dma((5, 2, 7)),
            dma((5, 2, 7)),
            dma((10,)),
            dma((10,)),
            dma((4,)),
            dma((4,)),
            dma((2, 4)),
            dma((2, 4)),
            dma((2, 7)),
            dma((2, 7)),
        ],
        compiler_params=pltpu.CompilerParams(
            collective_id=0, has_side_effects=True, vmem_limit_bytes=56 * 1024 * 1024
        ),
    )(
        grad_parts[0, 0], first_moment[0, 0], second_moment[0, 0], left_stat[0, 0],
        right_stat[0, 0], left_basis[0, 0], right_basis[0, 0], gain_grads[0, 0, 0],
        gain_first[0], gain_second[0], table_grads[0, 0], table_first, table_second,
    )
    return tuple(
        [value[None, None] for value in outs[:7]] + [value[None] for value in outs[7:10]]
        + list(outs[10:])
    )


def solution(mesh):
    return jax.shard_map(
        local,
        mesh=mesh,
        in_specs=(
            P("section", "dp", None, None, "tensor"),
            P("section", "tensor", "dp", None),
            P("section", "tensor", "dp", None),
            P("section", "tensor", "dp", None),
            P("section", "tensor", "dp", None),
            P("section", "tensor", "dp", None),
            P("section", "tensor", "dp", None),
            P("section", "dp", "tensor", None, None),
            P("section", None, None),
            P("section", None, None),
            P("section", "dp", None, "tensor"),
            P(None, "tensor"),
            P(None, "tensor"),
        ),
        out_specs=(
            P("section", "tensor", "dp", None),
            P("section", "tensor", "dp", None),
            P("section", "tensor", "dp", None),
            P("section", "tensor", "dp", None),
            P("section", "tensor", "dp", None),
            P("section", "tensor", "dp", None),
            P("section", "tensor", "dp", None),
            P("section", None, None),
            P("section", None, None),
            P("section", None, None),
            P(None, "tensor"),
            P(None, "tensor"),
            P(None, "tensor"),
        ),
        check_vma=False,
    )
```

```python
import jax
import jax.numpy as jnp
from jax import lax
from jax.experimental import pallas as pl
from jax.experimental.pallas import tpu as pltpu
from jax.sharding import PartitionSpec as P

MESH = pl.DeviceIdType.MESH
F32, BF16 = jnp.float32, jnp.bfloat16

beta_first = 0.9
beta_second = 0.95
beta_stat = 0.95
adam_eps = 1e-08
norm_eps = 1e-06
step_count = 10.0

D = 1024
NZ = 8
BLK = D // NZ
ROWS = BLK // 2
COLS = D // 4
HALF = D // 2
TILE = 256


def adam_direction(first, second):
    first_hat = first / (1.0 - beta_first**step_count)
    second_hat = second / (1.0 - beta_second**step_count)
    return first_hat / (jnp.sqrt(second_hat) + adam_eps)


def dot_nn(a, b):
    return jnp.dot(a, b, preferred_element_type=F32)


def dot_nt(a, b):
    return lax.dot_general(a, b, (((1,), (1,)), ((), ())), preferred_element_type=F32)


def dot_tn(a, b):
    return lax.dot_general(a, b, (((0,), (0,)), ((), ())), preferred_element_type=F32)


def wrap(value, size):
    return lax.rem(value + 2 * size, size)


def kernel(
    g_hbm, m1_hbm, m2_hbm, ls_hbm, rs_hbm, lb_hbm, rb_hbm, gg, gf, gs, tg, tf, ts,
    o_update, o_first, o_second, o_left, o_right, o_lrot, o_rrot,
    o_gu, o_gm, o_gs, o_tu, o_tm, o_ts,
    g, m1, m2, ls, rs, lb, rb,
    v_update, v_first, v_second, v_left, v_right, v_lrot, v_rrot,
    left128, basis_send, basis, grad, xhalf, xa, xb, gram, xf, ehalf,
    rs_recv, rs_send, zsum, ysum, gx, stat_recv, next_half,
    s_buf, rot, rot_send, rot_recv, d128, e_send, upd_send, upd_recv, fin_send, fin_recv,
    gain_x, gain_y, gain_ys, gain_z, tab_s, tab_y, tab_ys, tab_z,
    in_sem, out_sem, red_ss, red_rs,
    ring_ss, ring_rs, y_ss, y_rs, x_ss, x_rs, small_ss, small_rs, sring_ss, sring_rs,
):
    sources = [lb_hbm, rb_hbm, g_hbm, ls_hbm, rs_hbm, m1_hbm, m2_hbm]
    targets = [lb, rb, g, ls, rs, m1, m2]
    loads = [
        pltpu.make_async_copy(source, target, in_sem.at[i])
        for i, (source, target) in enumerate(zip(sources, targets))
    ]
    for load in loads:
        load.start()
    stores = []

    def emit(source, target):
        copy = pltpu.make_async_copy(source, target, out_sem.at[len(stores)])
        copy.start()
        stores.append(copy)

    dp = lax.axis_index("dp")
    x = lax.axis_index("tensor")
    sec = lax.axis_index("section")
    z = dp // 2
    y = lax.rem(dp, 2)
    up = {"dp": wrap(z + 1, NZ) * 2 + y}
    down = {"dp": wrap(z - 1, NZ) * 2 + y}
    partner = {"dp": z * 2 + 1 - y}
    pending = []

    def remote(src, dst, ssem, rsem, device):
        return pltpu.make_async_remote_copy(
            src_ref=src, dst_ref=dst, send_sem=ssem, recv_sem=rsem,
            device_id=device, device_id_type=MESH,
        )

    def send(*spec):
        copy = remote(*spec)
        copy.start()
        pending.append(copy)

    def xpeer(k):
        return {"tensor": lax.rem(x + k, 4)}

    def speer(k):
        return {"section": lax.rem(sec + k, 4)}

    barrier = pltpu.get_barrier_semaphore()
    peers = [up, down, partner] + [xpeer(k) for k in (1, 2, 3)] + [speer(k) for k in (1, 2, 3)]
    for peer in peers:
        pl.semaphore_signal(barrier, inc=1, device_id=peer, device_id_type=MESH)
    pl.semaphore_wait(barrier, len(peers))

    def rows(block, sub):
        return pl.ds(pl.multiple_of(block * BLK + sub * ROWS, ROWS), ROWS)

    def blk(block):
        return pl.ds(pl.multiple_of(block * BLK, BLK), BLK)

    mine = blk(z)
    own_sub = pl.ds(pl.multiple_of(y * ROWS, ROWS), ROWS)
    other_sub = pl.ds(pl.multiple_of((1 - y) * ROWS, ROWS), ROWS)

    def ring_spec(phase, buf, direction, m, at_sender):
        step = m // 2
        swapped = (m % 2 == 1) if m < 6 else (direction == 1)
        sub = (1 - y) if swapped else y
        sign = -1 if direction == 0 else 1
        origin = z if at_sender else z + sign
        block = wrap(origin + sign * step, NZ)
        part = buf.at[rows(block, sub), :]
        device = up if direction == 0 else down
        return (
            part, part, ring_ss.at[phase, direction, m], ring_rs.at[phase, direction, m], device,
        )

    def ring_send(phase, buf, m):
        for direction in (0, 1):
            send(*ring_spec(phase, buf, direction, m, True))

    def ring_step(phase, buf, m):
        for direction in (0, 1):
            remote(*ring_spec(phase, buf, direction, m, False)).wait_recv()
            if m < 4:
                send(*ring_spec(phase, buf, direction, m + 2, True))
            elif m == 4 + direction:
                send(*ring_spec(phase, buf, direction, 6, True))

    def rs_chunk(direction, step):
        return wrap(z - 1 - step if direction == 0 else z + 1 + step, NZ)

    def rs_copy(direction, chain, step, src):
        return (
            src, rs_recv.at[direction, step, chain], red_ss.at[direction, chain, step],
            red_rs.at[direction, chain, step], up if direction == 0 else down,
        )

    for chain in (0, 1):
        for direction in (0, 1):
            first = g_hbm.at[2 * direction + chain, blk(rs_chunk(direction, 0)), :]
            send(*rs_copy(direction, chain, 0, first))

    loads[0].wait()
    loads[1].wait()
    lhalf = lb[...].astype(BF16)
    rhalf = rb[...].astype(BF16)
    left128[own_sub, :] = lhalf

    @pl.when(y == 0)
    def _():
        basis[rows(z, 0), :] = lhalf
        basis_send[...] = rhalf

    @pl.when(y == 1)
    def _():
        basis[rows(z, 1), :] = rhalf
        basis_send[...] = lhalf

    send(basis_send, basis.at[rows(z, y), :], y_ss.at[0], y_rs.at[0], partner)
    ring_send(1, basis, 0)

    for k in (1, 2, 3):
        send(gg, gain_x.at[x], small_ss.at[0, k], small_rs.at[0, k], xpeer(k))
        send(tg, tab_s.at[sec], small_ss.at[1, k], small_rs.at[1, k], speer(k))
    gain_x[x] = gg[...]
    tab_s[sec] = tg[...]

    def stat_copy(src):
        return remote(src, stat_recv, y_ss.at[2], y_rs.at[2], partner)

    @pl.when(y == 0)
    def _():
        stat_copy(rs_hbm).start()

    @pl.when(y == 1)
    def _():
        stat_copy(ls_hbm).start()

    pending.append(stat_copy(ls_hbm))
    send(left128.at[own_sub, :], left128.at[own_sub, :], y_ss.at[1], y_rs.at[1], partner)
    remote(basis_send, basis.at[rows(z, 1 - y), :], y_ss.at[0], y_rs.at[0], partner).wait_recv()
    ring_send(1, basis, 1)
    loads[2].wait()

    def swap_spec(mat):
        return (zsum.at[mat], ysum.at[mat], y_ss.at[10 + mat], y_rs.at[10 + mat], partner)

    for m in range(7):
        for chain in (0, 1):
            for direction in (0, 1):
                mat = 2 * direction + chain
                landed = rs_recv.at[direction, m, chain]
                remote(*rs_copy(direction, chain, m, landed)).wait_recv()
                own = g[mat, blk(rs_chunk(direction, m + 1)), :].astype(F32)
                total = (landed[...].astype(F32) + own).astype(BF16)
                if m < 6:
                    rs_send[direction, m, chain] = total
                    send(*rs_copy(direction, chain, m + 1, rs_send.at[direction, m, chain]))
                else:
                    zsum[mat] = total
                    send(*swap_spec(mat))
        if m in (2, 4):
            ring_step(1, basis, m // 2 - 1)
    ring_step(1, basis, 2)

    def cols(rank):
        return pl.ds(pl.multiple_of(rank * COLS, COLS), COLS)

    for chain in (0, 1):
        for direction in (0, 1):
            mat = 2 * direction + chain
            remote(*swap_spec(mat)).wait_recv()
            gx[mat] = (zsum[mat].astype(F32) + ysum[mat].astype(F32)).astype(BF16)

            @pl.when(x == mat)
            def _(mat=mat):
                grad[mine, cols(x)] = gx[mat]

            @pl.when(x != mat)
            def _(mat=mat):
                k = wrap(mat - x, 4)
                remote(
                    gx.at[mat], grad.at[mine, cols(x)], x_ss.at[k], x_rs.at[k], {"tensor": mat}
                ).start()

    for k in (1, 2, 3):
        pending.append(
            remote(gx.at[0], grad.at[mine, cols(x)], x_ss.at[k], x_rs.at[k], xpeer(k))
        )
    ring_step(1, basis, 3)
    ring_step(1, basis, 4)

    for k in (1, 2, 3):
        source = wrap(x - k, 4)
        remote(gg, gain_x.at[source], small_ss.at[0, k], small_rs.at[0, k], xpeer(k)).wait_recv()
        source = wrap(sec - k, 4)
        remote(tg, tab_s.at[source], small_ss.at[1, k], small_rs.at[1, k], speer(k)).wait_recv()
    gain_ys[...] = gain_x[0] + gain_x[1] + gain_x[2] + gain_x[3]
    tab_ys[...] = tab_s[0] + tab_s[1] + tab_s[2] + tab_s[3]
    send(gain_ys, gain_y, small_ss.at[0, 0], small_rs.at[0, 0], partner)
    send(tab_ys, tab_y, small_ss.at[1, 0], small_rs.at[1, 0], partner)

    for k in (1, 2, 3):
        part = grad.at[mine, cols(wrap(x - k, 4))]
        remote(gx.at[0], part, x_ss.at[k], x_rs.at[k], xpeer(k)).wait_recv()

    ring_send(2, grad, 0)
    ring_send(2, grad, 1)
    ring_step(1, basis, 5)
    remote(gain_ys, gain_y, small_ss.at[0, 0], small_rs.at[0, 0], partner).wait_recv()
    remote(tab_ys, tab_y, small_ss.at[1, 0], small_rs.at[1, 0], partner).wait_recv()
    gain_z[z] = gain_ys[...] + gain_y[...]
    tab_z[z] = tab_ys[...] + tab_y[...]

    def small_ring(m, at_sender):
        origin = z if at_sender else z - 1
        slot = wrap(origin - m, NZ)
        first = (gain_z.at[slot], gain_z.at[slot], sring_ss.at[0, m], sring_rs.at[0, m], up)
        second = (tab_z.at[slot], tab_z.at[slot], sring_ss.at[1, m], sring_rs.at[1, m], up)
        return first, second

    for m in range(7):
        ring_step(2, grad, m)
        if m == 2:
            ring_step(1, basis, 6)

    remote(ls_hbm, stat_recv, y_ss.at[2], y_rs.at[2], partner).wait_recv()
    for load in loads[3:]:
        load.wait()

    @pl.when(y == 0)
    def _():
        prod = dot_nt(grad[mine, :], grad[...])
        top = beta_stat * ls[...] + prod[:ROWS]
        v_left[...] = top
        next_half[:ROWS] = top.astype(BF16)
        next_half[ROWS:] = (beta_stat * stat_recv[...] + prod[ROWS:]).astype(BF16)

    @pl.when(y == 1)
    def _():
        prod = dot_tn(grad[:, mine], grad[...])
        bottom = beta_stat * rs[...] + prod[ROWS:]
        v_right[...] = bottom
        next_half[:ROWS] = (beta_stat * stat_recv[...] + prod[:ROWS]).astype(BF16)
        next_half[ROWS:] = bottom.astype(BF16)

    xhalf[mine, :] = dot_nn(next_half[...], basis[...]).astype(BF16)
    ring_send(3, xhalf, 0)
    ring_send(3, xhalf, 1)

    s_copy = remote(s_buf, s_buf, y_ss.at[4], y_rs.at[4], partner)
    rot_copy = remote(rot_send, rot_recv, y_ss.at[5], y_rs.at[5], partner)
    d_copy = remote(
        d128.at[pl.ds(0, ROWS), :], d128.at[pl.ds(0, ROWS), :], y_ss.at[6], y_rs.at[6], partner
    )
    e_copy = remote(e_send, ehalf.at[mine, :], y_ss.at[7], y_rs.at[7], partner)

    for spec in small_ring(0, True):
        send(*spec)

    def small_step(m):
        for spec in small_ring(m, False):
            remote(*spec).wait_recv()
        if m < 6:
            for spec in small_ring(m + 1, True):
                send(*spec)

    @pl.when(y == 0)
    def _():
        s_buf[...] = dot_tn(basis[:, mine], grad[...]).astype(BF16)
        s_copy.start()
        prod = dot_tn(grad[:, mine], grad[...])
        v_right[...] = beta_stat * rs[...] + prod[:ROWS]

    @pl.when(y == 1)
    def _():
        prod = dot_nt(grad[rows(z, 1), :], grad[...])
        v_left[...] = beta_stat * ls[...] + prod

    emit(v_left, o_left)
    emit(v_right, o_right)
    ring_step(3, xhalf, 0)
    small_step(0)
    ring_step(3, xhalf, 1)
    small_step(1)
    ring_step(3, xhalf, 2)

    @pl.when(y == 1)
    def _():
        s_copy.wait_recv()
        rotated = dot_nn(s_buf[...], basis[...])
        rot_send[...] = rotated[:ROWS].astype(BF16)
        rot_copy.start()
        rot[...] = rotated[ROWS:]

    small_step(2)
    ring_step(3, xhalf, 3)
    small_step(3)
    ring_step(3, xhalf, 4)

    @pl.when(y == 0)
    def _():
        rot_copy.wait_recv()
        rot[...] = rot_recv[...].astype(F32)

    rotated = rot[...]
    first_new = beta_first * m1[...] + (1.0 - beta_first) * rotated
    second_new = beta_second * m2[...] + (1.0 - beta_second) * rotated * rotated
    v_first[...] = first_new
    v_second[...] = second_new
    d128[own_sub, :] = adam_direction(first_new, second_new).astype(BF16)

    @pl.when(y == 0)
    def _():
        d_copy.start()

    emit(v_first, o_first)
    emit(v_second, o_second)
    small_step(4)
    ring_step(3, xhalf, 5)
    small_step(5)
    ring_step(3, xhalf, 6)

    @pl.when(y == 1)
    def _():
        d_copy.wait_recv()
        e_send[...] = dot_nt(d128[...], basis[pl.ds(0, HALF), :]).astype(BF16)
        e_copy.start()
        ehalf[mine, :] = dot_nt(d128[...], basis[pl.ds(HALF, HALF), :]).astype(BF16)

    def tile(i):
        return pl.ds(pl.multiple_of(i * TILE, TILE), TILE)

    def squares(i, acc):
        part = xhalf[tile(i), :].astype(F32)
        return acc + jnp.sum((part * part).reshape(TILE // 8, 8, D), axis=0)

    partial = lax.fori_loop(0, D // TILE, squares, jnp.zeros((8, D), F32))
    scale = 1.0 / jnp.sqrt(jnp.sum(partial, keepdims=True) + norm_eps)

    @pl.loop(0, D // TILE)
    def _(i):
        value = xhalf[tile(i), :].astype(F32) * scale
        xf[tile(i), :] = value
        xa[tile(i), :] = value.astype(BF16)

    def gram_pass(source, half):
        @pl.loop(2 * half, 2 * half + 2)
        def _(i):
            gram[tile(i), :] = dot_nt(source[tile(i), :], source[...]).astype(BF16)

    def apply_pass(source, target, half):
        @pl.loop(2 * half, 2 * half + 2)
        def _(i):
            value = 1.5 * xf[tile(i), :] - 0.5 * dot_nn(gram[tile(i), :], source[...])
            xf[tile(i), :] = value
            target[tile(i), :] = value.astype(BF16)

    gram_pass(xa, 0)

    @pl.when(y == 0)
    def _():
        e_copy.wait_recv()

    ring_send(4, ehalf, 0)
    ring_send(4, ehalf, 1)
    small_step(6)
    gram_pass(xa, 1)
    apply_pass(xa, xb, 0)
    ring_step(4, ehalf, 0)
    apply_pass(xa, xb, 1)
    ring_step(4, ehalf, 1)
    gram_pass(xb, 0)
    ring_step(4, ehalf, 2)
    gram_pass(xb, 1)
    ring_step(4, ehalf, 3)
    apply_pass(xb, xa, 0)
    ring_step(4, ehalf, 4)
    apply_pass(xb, xa, 1)
    ring_step(4, ehalf, 5)

    gram_own = dot_nt(xa[mine, :], xa[...]).astype(BF16)
    final = 1.5 * xf[mine, :] - 0.5 * dot_nn(gram_own, xa[...])

    @pl.when(y == 0)
    def _():
        v_lrot[...] = final[:ROWS]
        fin_send[...] = final[ROWS:].astype(BF16)

    @pl.when(y == 1)
    def _():
        v_rrot[...] = final[ROWS:]
        fin_send[...] = final[:ROWS].astype(BF16)

    send(fin_send, fin_recv, y_ss.at[8], y_rs.at[8], partner)
    ring_step(4, ehalf, 6)

    remote(
        left128.at[own_sub, :], left128.at[other_sub, :], y_ss.at[1], y_rs.at[1], partner
    ).wait_recv()

    @pl.when(y == 0)
    def _():
        upd = dot_nn(left128[...], ehalf[...])
        v_update[:, :HALF] = upd[:ROWS]
        upd_send[...] = upd[ROWS:].astype(BF16)

    @pl.when(y == 1)
    def _():
        upd = dot_nn(left128[...], ehalf[...])
        v_update[:, HALF:] = upd[ROWS:]
        upd_send[...] = upd[:ROWS].astype(BF16)

    send(upd_send, upd_recv, y_ss.at[9], y_rs.at[9], partner)

    def total_of(slots):
        total = slots[0]
        for k in range(1, NZ):
            total = total + slots[k]
        return total

    gain_sum = total_of(gain_z)
    gain_moment = beta_first * gf[...] + (1.0 - beta_first) * gain_sum
    gain_squares = beta_second * gs[...] + (1.0 - beta_second) * gain_sum * gain_sum
    o_gm[...] = gain_moment
    o_gs[...] = gain_squares
    o_gu[...] = adam_direction(gain_moment, gain_squares)
    table_sum = total_of(tab_z)
    table_moment = beta_first * tf[...] + (1.0 - beta_first) * table_sum
    table_squares = beta_second * ts[...] + (1.0 - beta_second) * table_sum * table_sum
    o_tm[...] = table_moment
    o_ts[...] = table_squares
    o_tu[...] = adam_direction(table_moment, table_squares)

    remote(fin_send, fin_recv, y_ss.at[8], y_rs.at[8], partner).wait_recv()

    @pl.when(y == 0)
    def _():
        v_rrot[...] = fin_recv[...].astype(F32)

    @pl.when(y == 1)
    def _():
        v_lrot[...] = fin_recv[...].astype(F32)

    emit(v_lrot, o_lrot)
    emit(v_rrot, o_rrot)
    remote(upd_send, upd_recv, y_ss.at[9], y_rs.at[9], partner).wait_recv()

    @pl.when(y == 0)
    def _():
        v_update[:, HALF:] = upd_recv[...].astype(F32)
        s_copy.wait_send()
        d_copy.wait_send()

    @pl.when(y == 1)
    def _():
        v_update[:, :HALF] = upd_recv[...].astype(F32)
        rot_copy.wait_send()
        e_copy.wait_send()

    emit(v_update, o_update)
    for copy in pending:
        copy.wait_send()
    for copy in stores:
        copy.wait()


def write_out(*refs):
    n = 13
    ins, outs, bufs, (in_sem, out_sem) = refs[:n], refs[n : 2 * n], refs[2 * n : 3 * n], refs[3 * n :]
    loads = [pltpu.make_async_copy(ins[i], bufs[i], in_sem.at[i]) for i in range(n)]
    stores = [pltpu.make_async_copy(bufs[i], outs[i], out_sem.at[i]) for i in range(n)]
    for load in loads:
        load.start()
    for load, store in zip(loads, stores):
        load.wait()
        store.start()
    for store in stores:
        store.wait()


def local(
    grad_parts, first_moment, second_moment, left_stat, right_stat, left_basis, right_basis,
    gain_grads, gain_first, gain_second, table_grads, table_first, table_second,
):
    wide = jax.ShapeDtypeStruct((ROWS, D), F32)
    gain = jax.ShapeDtypeStruct((2, D), F32)
    table = jax.ShapeDtypeStruct((4, 32), F32)
    shapes = [wide] * 7 + [gain] * 3 + [table] * 3
    vmem = pl.BlockSpec(memory_space=pltpu.VMEM)
    hbm = pl.BlockSpec(memory_space=pl.ANY)
    dma = pltpu.SemaphoreType.DMA
    outs = pl.pallas_call(
        kernel,
        out_shape=shapes,
        in_specs=[hbm] * 7 + [vmem] * 6,
        out_specs=[hbm] * 7 + [vmem] * 6,
        scratch_shapes=[
            pltpu.VMEM((4, D, COLS), BF16),
            *[pltpu.VMEM((ROWS, D), F32)] * 6,
            *[pltpu.VMEM((ROWS, D), F32)] * 7,
            pltpu.VMEM((BLK, D), BF16),
            pltpu.VMEM((ROWS, D), BF16),
            pltpu.VMEM((D, D), BF16),
            pltpu.VMEM((D, D), BF16),
            pltpu.VMEM((D, D), BF16),
            pltpu.VMEM((D, D), BF16),
            pltpu.VMEM((D, D), BF16),
            pltpu.VMEM((D, D), BF16),
            pltpu.VMEM((D, D), F32),
            pltpu.VMEM((D, HALF), BF16),
            pltpu.VMEM((2, 7, 2, BLK, COLS), BF16),
            pltpu.VMEM((2, 6, 2, BLK, COLS), BF16),
            pltpu.VMEM((4, BLK, COLS), BF16),
            pltpu.VMEM((4, BLK, COLS), BF16),
            pltpu.VMEM((4, BLK, COLS), BF16),
            pltpu.VMEM((ROWS, D), F32),
            pltpu.VMEM((BLK, D), BF16),
            pltpu.VMEM((BLK, D), BF16),
            pltpu.VMEM((ROWS, D), F32),
            pltpu.VMEM((ROWS, D), BF16),
            pltpu.VMEM((ROWS, D), BF16),
            pltpu.VMEM((BLK, D), BF16),
            pltpu.VMEM((BLK, HALF), BF16),
            pltpu.VMEM((ROWS, HALF), BF16),
            pltpu.VMEM((ROWS, HALF), BF16),
            pltpu.VMEM((ROWS, D), BF16),
            pltpu.VMEM((ROWS, D), BF16),
            pltpu.VMEM((4, 2, D), F32),
            pltpu.VMEM((2, D), F32),
            pltpu.VMEM((2, D), F32),
            pltpu.VMEM((NZ, 2, D), F32),
            pltpu.VMEM((4, 4, 32), F32),
            pltpu.VMEM((4, 32), F32),
            pltpu.VMEM((4, 32), F32),
            pltpu.VMEM((NZ, 4, 32), F32),
            dma((7,)),
            dma((7,)),
            dma((2, 2, 7)),
            dma((2, 2, 7)),
            dma((5, 2, 7)),
            dma((5, 2, 7)),
            dma((14,)),
            dma((14,)),
            dma((4,)),
            dma((4,)),
            dma((2, 4)),
            dma((2, 4)),
            dma((2, 7)),
            dma((2, 7)),
        ],
        compiler_params=pltpu.CompilerParams(
            collective_id=0, has_side_effects=True, vmem_limit_bytes=56 * 1024 * 1024
        ),
    )(
        grad_parts[0, 0], first_moment[0, 0], second_moment[0, 0], left_stat[0, 0],
        right_stat[0, 0], left_basis[0, 0], right_basis[0, 0], gain_grads[0, 0, 0],
        gain_first[0], gain_second[0], table_grads[0, 0].T, table_first.T, table_second.T,
    )
    outs = pl.pallas_call(
        write_out,
        out_shape=shapes,
        in_specs=[hbm] * 13,
        out_specs=[hbm] * 13,
        scratch_shapes=[*[pltpu.VMEM(s.shape, s.dtype) for s in shapes], dma((13,)), dma((13,))],
    )(*outs)
    return tuple(
        [value[None, None] for value in outs[:7]] + [value[None] for value in outs[7:10]]
        + [value.T for value in outs[10:]]
    )


def solution(mesh):
    return jax.shard_map(
        local,
        mesh=mesh,
        in_specs=(
            P("section", "dp", None, None, "tensor"),
            P("section", "tensor", "dp", None),
            P("section", "tensor", "dp", None),
            P("section", "tensor", "dp", None),
            P("section", "tensor", "dp", None),
            P("section", "tensor", "dp", None),
            P("section", "tensor", "dp", None),
            P("section", "dp", "tensor", None, None),
            P("section", None, None),
            P("section", None, None),
            P("section", "dp", None, "tensor"),
            P(None, "tensor"),
            P(None, "tensor"),
        ),
        out_specs=(
            P("section", "tensor", "dp", None),
            P("section", "tensor", "dp", None),
            P("section", "tensor", "dp", None),
            P("section", "tensor", "dp", None),
            P("section", "tensor", "dp", None),
            P("section", "tensor", "dp", None),
            P("section", "tensor", "dp", None),
            P("section", None, None),
            P("section", None, None),
            P("section", None, None),
            P(None, "tensor"),
            P(None, "tensor"),
            P(None, "tensor"),
        ),
        check_vma=False,
    )
```
